128 devices in a mesh: replica: 16 (over y_hi, x, core), tensor: 8 (over z, y_lo).
Axes of the slice: x: 4, y: 4 (y_hi: 2, y_lo: 2; y = y_hi * 2 + y_lo), z: 4, core: 2. Of those that a mesh axis runs over, the one named last changes fastest.
Arguments:
- hidden: bfloat16 [4096, 14336], P('replica', 'tensor'), may hold values from -6 to 6
- out_grad: bfloat16 [4096, 4096], P(('replica', 'tensor')), may hold values from -6 to 6
- weights: bfloat16 [16, 112, 128, 1024], P('replica', 'tensor'), may hold values from -6 to 6
- momentum: bfloat16 [16, 112, 128, 1024], P('replica', 'tensor'), may hold values from -3 to 3
- block_cols: int32 [112, 8], P('tensor'), may hold values from 0 to 31, as said below
- step_number: int32 [1], replicated, may hold values from 0 to 999
Outputs:
- outputs: bfloat16 [4096, 4096], P(('replica', 'tensor'))
- new_weights: bfloat16 [16, 112, 128, 1024], P('replica', 'tensor')
- new_momentum: bfloat16 [16, 112, 128, 1024], P('replica', 'tensor')
The draws below stay inside these ranges and needn't reach their ends.
Inputs may be any that keep to these rules, and one draw needn't show every extreme that they name: `block_cols`: each row names 8 different column blocks; all replicas share the pattern.
All inputs are finite; a program needn't handle non-finite values.
Results may differ from the reference program's by a relative error of at most 0.013.
Values may be sent and summed in bfloat16 or wider, within the bound.
A program may use at most 192 MiB of HBM per device.

```python
import jax
import jax.numpy as jnp
from jax import lax

D = 4096
BLOCK = 128
TOK = 256
KB = 8
FF = 14336
TOKENS = 4096
N_REPLICA = 16
N_TENSOR = 8


def draw_block_cols(key, part):
    row_total = FF // BLOCK
    keys = jax.random.split(jax.random.fold_in(key, 17), row_total)

    def pick_row(row_key):
        return jax.random.permutation(row_key, D // BLOCK)[:KB]
    return jax.vmap(pick_row)(keys).astype(jnp.int32)


def level_of(own_key, dims, cuts, smallest, high):
    factor_of, own = 1.0, jax.random.fold_in(own_key, 6)
    for axis_at, shards_of in cuts:
        draws = jnp.exp(jax.random.uniform(jax.random.fold_in(own, axis_at), (shards_of,), jnp.float32, smallest / len(cuts), high / len(cuts)))
        factor_of = factor_of * jnp.repeat(draws, dims[axis_at] // shards_of).reshape([-1 if axis == axis_at else 1 for axis in range(len(dims))])
    return factor_of


def scatter_about(key, shape, deviation, limit, cuts=(), held_as=jnp.bfloat16):
    drawn = deviation * jax.random.normal(key, shape, jnp.float32)
    if cuts:
        drawn = drawn * level_of(key, shape, cuts, -0.22, 0.18)
    return jnp.clip(drawn, -limit, limit).astype(held_as)


def setup_inputs(seed: int = 0) -> dict:
    key_of = jax.random.split(jax.random.key(seed), 7)
    return {
        "hidden": scatter_about(key_of[0], (TOKENS, FF), 1.0, 6.0, ((0, 16), (1, 8))),
        "out_grad": scatter_about(key_of[1], (TOKENS, D), 1.0, 6.0, ((0, 128),)),
        "weights": scatter_about(key_of[2], (N_REPLICA, FF // BLOCK, BLOCK, KB * BLOCK), 1.0, 6.0, ((0, 16), (1, 8))),
        "momentum": scatter_about(key_of[3], (N_REPLICA, FF // BLOCK, BLOCK, KB * BLOCK), 0.5, 3.0, ((0, 16), (1, 8))),
        "block_cols": draw_block_cols(jax.random.fold_in(key_of[6], 71), 0),
        "step_number": jax.random.randint(key_of[5], (1,), 0, 1000).astype(jnp.int32),
    }


LAMBDA_DC = 1.0
MOMENT_DECAY = 0.9
LEARN_RATE = 0.2


def replica_pass(hidden_rows, grad_rows, local_weights, block_cols, weight_scale):
    col_blocks = D // BLOCK
    row_total = FF // BLOCK
    hid_blocks = hidden_rows.reshape(TOK, row_total, BLOCK)
    grad_blocks = grad_rows.reshape(TOK, col_blocks, BLOCK)

    def row_block(position):
        hid_piece = lax.dynamic_index_in_dim(hid_blocks, position, 1, keepdims=False)
        weight_piece = lax.dynamic_index_in_dim(local_weights, position, 0, keepdims=False)
        columns = lax.dynamic_index_in_dim(block_cols, position, 0, keepdims=False)
        product = jnp.dot(hid_piece, weight_piece, preferred_element_type=jnp.float32) * weight_scale
        selected = jnp.take(grad_blocks, columns, axis=1).reshape(TOK, KB * BLOCK)
        gradient = jnp.dot(hid_piece.T, selected, preferred_element_type=jnp.float32)
        return product, gradient

    products, gradients = lax.map(row_block, jnp.arange(row_total, dtype=jnp.int32))
    moved = products.reshape(row_total, TOK, KB, BLOCK).transpose(0, 2, 1, 3)
    shard_of = (jnp.arange(row_total, dtype=jnp.int32) // (row_total // N_TENSOR))[:, None]
    parts = jnp.zeros((N_TENSOR, col_blocks, TOK, BLOCK), jnp.float32).at[shard_of, block_cols].add(moved)
    parts = lax.optimization_barrier(parts.astype(jnp.bfloat16)).astype(jnp.float32)
    summed = jnp.sum(parts, axis=0).transpose(1, 0, 2).reshape(TOK, D)
    return summed.astype(jnp.bfloat16), gradients * weight_scale


def reference(hidden, out_grad, weights, momentum, block_cols, step_number):
    weight_scale = (4.0 / FF) ** 0.5

    def per_replica(items):
        return replica_pass(items[0], items[1], items[2], block_cols, weight_scale)

    outputs, gradients = lax.map(per_replica, (hidden.reshape(N_REPLICA, TOK, FF), out_grad.reshape(N_REPLICA, TOK, D), weights))
    level_count = N_REPLICA.bit_length() - 1
    chosen_bit = step_number[0] % level_count
    position = jnp.arange(N_REPLICA, dtype=jnp.int32)
    partner = jnp.bitwise_xor(position, jnp.left_shift(jnp.ones((), jnp.int32), chosen_bit.astype(jnp.int32)))
    own_w = weights.astype(jnp.float32)
    own_m = momentum.astype(jnp.float32)
    mate_w = weights[partner].astype(jnp.float32)
    mate_m = momentum[partner].astype(jnp.float32)
    mean_w = 0.5 * (own_w + mate_w)
    mean_m = 0.5 * (own_m + mate_m)
    corrected = gradients + LAMBDA_DC * gradients * gradients * (mean_w - own_w)
    moment_new = MOMENT_DECAY * mean_m + corrected
    weight_new = mean_w - LEARN_RATE * moment_new
    return outputs.reshape(TOKENS, D), weight_new.astype(jnp.bfloat16), moment_new.astype(jnp.bfloat16)
```

```python
import functools

import jax
import jax.numpy as jnp
from jax import lax
from jax.experimental import pallas as pl
from jax.experimental.pallas import tpu as pltpu
from jax.sharding import PartitionSpec as P

LAMBDA_DC = 1.0
MOMENT_DECAY = 0.9
LEARN_RATE = 0.2
MESH = pl.DeviceIdType.MESH


def step_kernel(
    bit,
    n_z,
    scale,
    cols_ref,
    inv_ref,
    hid_hbm,
    og_hbm,
    w_hbm,
    m_hbm,
    out_hbm,
    nw_hbm,
    nm_hbm,
    hid_v,
    w_v,
    m_v,
    wp_v,
    mp_v,
    sec_v,
    sec_c,
    wd_v,
    part_v,
    rs_v,
    keep_v,
    ysend_v,
    yrecv_v,
    out_v,
    nw_v,
    nm_v,
    ld_sem,
    g_send,
    g_recv,
    ag_send,
    ag_recv,
    rs_send,
    rs_recv,
    y_send,
    y_recv,
    o_sem,
    wo_sem,
):
    row_blocks, block, width = w_hbm.shape
    rows_here, model_width = og_hbm.shape
    col_blocks = model_width // block
    per_row = width // block
    replica = lax.axis_index("replica")
    tensor = lax.axis_index("tensor")
    z, y_lo = tensor // 2, tensor % 2
    low = (replica // (1 << bit)) % 2
    partner = replica + (1 - 2 * low) * (1 << bit)
    y_mate = z * 2 + (1 - y_lo)
    z_mates = [lax.rem(z + d, n_z) for d in range(1, n_z)]

    loads = [
        pltpu.make_async_copy(hid_hbm, hid_v, ld_sem.at[0]),
        pltpu.make_async_copy(
            og_hbm, sec_v.at[pl.ds(tensor * rows_here, rows_here)], ld_sem.at[1]
        ),
        pltpu.make_async_copy(m_hbm, m_v, ld_sem.at[2]),
    ]
    loads += [
        pltpu.make_async_copy(
            w_hbm.at[:, :, pl.ds(k * block, block)], w_v.at[:, k], ld_sem.at[3 + k]
        )
        for k in range(per_row)
    ]
    for copy in loads:
        copy.start()

    barrier = pltpu.get_barrier_semaphore()
    pl.semaphore_signal(
        barrier, inc=1, device_id={"replica": partner}, device_id_type=MESH
    )
    for peer in [y_mate] + [zz * 2 + y_lo for zz in z_mates]:
        pl.semaphore_signal(
            barrier, inc=1, device_id={"tensor": peer}, device_id_type=MESH
        )
    pl.semaphore_wait(barrier, n_z + 1)

    def gather_copy(src, owner, peer, slot, recv):
        return pltpu.make_async_remote_copy(
            src_ref=src,
            dst_ref=sec_v.at[pl.ds(owner * rows_here, rows_here)],
            send_sem=ag_send.at[slot],
            recv_sem=ag_recv.at[recv],
            device_id={"tensor": peer},
            device_id_type=MESH,
        )

    first = [gather_copy(og_hbm, tensor, y_mate, 0, 0)]
    for d in range(1, n_z):
        first.append(
            gather_copy(og_hbm, tensor, z_mates[d - 1] * 2 + y_lo, d, 2 * d - 1)
        )
    for copy in first:
        copy.start()

    def gossip(r):
        pair = []
        for a, (src, dst) in enumerate(((w_hbm, wp_v), (m_hbm, mp_v))):
            pair.append(
                pltpu.make_async_remote_copy(
                    src_ref=src.at[r],
                    dst_ref=dst.at[r],
                    send_sem=g_send.at[a, r],
                    recv_sem=g_recv.at[a, r],
                    device_id={"replica": partner},
                    device_id_type=MESH,
                )
            )
        return pair

    early = row_blocks // 2

    def start_gossip(r, carry):
        for copy in gossip(r):
            copy.start()
        return carry

    lax.fori_loop(0, early, start_gossip, 0)

    for r in range(row_blocks):
        w_v[r, per_row] = jnp.zeros((block, block), w_v.dtype)

    loads[0].wait()
    for copy in loads[3:]:
        copy.wait()
    pair_width = 2 * block

    def forward(c, carry):
        for r in range(row_blocks):
            for h in range(2):
                wd_v[pl.ds(r * block, block), pl.ds(h * block, block)] = w_v[
                    r, inv_ref[r, c * 2 + h]
                ]
        product = jnp.dot(hid_v[...], wd_v[...], preferred_element_type=jnp.float32)
        part_v[:, pl.ds(pl.multiple_of(c * pair_width, pair_width), pair_width)] = (
            product * scale
        ).astype(part_v.dtype)
        return carry

    lax.fori_loop(0, col_blocks // 2, forward, 0)

    first[0].wait_recv()
    second = []
    for d in range(1, n_z):
        second.append(
            gather_copy(
                sec_v.at[pl.ds(y_mate * rows_here, rows_here)],
                y_mate,
                z_mates[d - 1] * 2 + y_lo,
                n_z - 1 + d,
                2 * d,
            )
        )
    for copy in second:
        copy.start()

    z_rows = 2 * rows_here
    scatter = []
    for d in range(1, n_z):
        scatter.append(
            pltpu.make_async_remote_copy(
                src_ref=part_v.at[pl.ds(z_mates[d - 1] * z_rows, z_rows)],
                dst_ref=rs_v.at[d - 1],
                send_sem=rs_send.at[d - 1],
                recv_sem=rs_recv.at[d - 1],
                device_id={"tensor": z_mates[d - 1] * 2 + y_lo},
                device_id_type=MESH,
            )
        )
    for copy in scatter:
        copy.start()
    lax.fori_loop(early, row_blocks, start_gossip, 0)

    loads[1].wait()
    loads[2].wait()
    for copy in first[1:] + second:
        copy.wait_recv()
    for c in range(col_blocks):
        sec_c[c] = sec_v[:, pl.ds(c * block, block)]

    def update(r, carry):
        hid_t = hid_v[:, pl.ds(pl.multiple_of(r * block, block), block)].T
        for copy in gossip(r):
            copy.wait_recv()
        for k in range(0, per_row, 2):
            picked = [sec_c[cols_ref[k + h, r]] for h in range(2)]
            at = pl.ds(k * block, pair_width)
            grad = scale * jnp.dot(
                hid_t,
                jnp.concatenate(picked, axis=1),
                preferred_element_type=jnp.float32,
            )
            own_w = jnp.concatenate([w_v[r, k], w_v[r, k + 1]], axis=1)
            own_w = own_w.astype(jnp.float32)
            mean_w = 0.5 * (own_w + wp_v[r, :, at].astype(jnp.float32))
            mean_m = 0.5 * (
                m_v[r, :, at].astype(jnp.float32) + mp_v[r, :, at].astype(jnp.float32)
            )
            corrected = grad + LAMBDA_DC * grad * grad * (mean_w - own_w)
            moment = MOMENT_DECAY * mean_m + corrected
            nm_v[r, :, at] = moment.astype(nm_v.dtype)
            nw_v[r, :, at] = (mean_w - LEARN_RATE * moment).astype(nw_v.dtype)
        for copy in results(r):
            copy.start()
        return carry

    def results(r):
        return [
            pltpu.make_async_copy(nw_v.at[r], nw_hbm.at[r], wo_sem.at[0, r]),
            pltpu.make_async_copy(nm_v.at[r], nm_hbm.at[r], wo_sem.at[1, r]),
        ]

    stop_a = row_blocks // 4
    stop_b = row_blocks - 3
    lax.fori_loop(0, stop_a, update, 0)

    for copy in scatter:
        copy.wait_recv()
    other = 1 - y_lo
    for dst, row in ((ysend_v, other), (keep_v, y_lo)):
        total = part_v[pl.ds(z * z_rows + row * rows_here, rows_here), :].astype(
            jnp.float32
        )
        for d in range(1, n_z):
            total += rs_v[d - 1, pl.ds(row * rows_here, rows_here), :].astype(
                jnp.float32
            )
        dst[...] = total.astype(dst.dtype)
    to_mate = pltpu.make_async_remote_copy(
        src_ref=ysend_v,
        dst_ref=yrecv_v,
        send_sem=y_send,
        recv_sem=y_recv,
        device_id={"tensor": y_mate},
        device_id_type=MESH,
    )
    to_mate.start()

    lax.fori_loop(stop_a, stop_b, update, 0)
    to_mate.wait_recv()
    out_v[...] = (keep_v[...] + yrecv_v[...].astype(jnp.float32)).astype(out_v.dtype)
    out_copy = pltpu.make_async_copy(out_v, out_hbm, o_sem)
    out_copy.start()
    lax.fori_loop(stop_b, row_blocks, update, 0)

    def finish(r, carry):
        for copy in gossip(r):
            copy.wait_send()
        for copy in results(r):
            copy.wait()
        return carry

    lax.fori_loop(0, row_blocks, finish, 0)
    for copy in first + second + scatter + [to_mate]:
        copy.wait_send()
    out_copy.wait()


def fused_step(bit, n_tensor, hidden, out_grad, weights, momentum, cols_t, places):
    token_count, unit_count = hidden.shape
    rows_here, model_width = out_grad.shape
    row_blocks, block, width = weights.shape
    n_z = n_tensor // 2
    scale = (4.0 / (unit_count * n_tensor)) ** 0.5
    b16, f32 = jnp.bfloat16, jnp.float32
    dma = pltpu.SemaphoreType.DMA
    any_spec = pl.BlockSpec(memory_space=pl.ANY)
    return pl.pallas_call(
        functools.partial(step_kernel, bit, n_z, scale),
        name=f"gossip_step_{bit}",
        out_shape=(
            jax.ShapeDtypeStruct(out_grad.shape, b16),
            jax.ShapeDtypeStruct(weights.shape, b16),
            jax.ShapeDtypeStruct(momentum.shape, b16),
        ),
        in_specs=[pl.BlockSpec(memory_space=pltpu.SMEM)] * 2 + [any_spec] * 4,
        out_specs=(any_spec,) * 3,
        scratch_shapes=[
            pltpu.VMEM((token_count, unit_count), b16),
            pltpu.VMEM((row_blocks, width // block + 1, block, block), b16),
            pltpu.VMEM((row_blocks, block, width), b16),
            pltpu.VMEM((row_blocks, block, width), b16),
            pltpu.VMEM((row_blocks, block, width), b16),
            pltpu.VMEM((token_count, model_width), b16),
            pltpu.VMEM((model_width // block, token_count, block), b16),
            pltpu.VMEM((unit_count, 2 * block), b16),
            pltpu.VMEM((token_count, model_width), b16),
            pltpu.VMEM((n_z - 1, 2 * rows_here, model_width), b16),
            pltpu.VMEM((rows_here, model_width), f32),
            pltpu.VMEM((rows_here, model_width), b16),
            pltpu.VMEM((rows_here, model_width), b16),
            pltpu.VMEM((rows_here, model_width), b16),
            pltpu.VMEM((row_blocks, block, width), b16),
            pltpu.VMEM((row_blocks, block, width), b16),
            dma((3 + width // block,)),
            dma((2, row_blocks)),
            dma((2, row_blocks)),
            dma((2 * n_z - 1,)),
            dma((2 * n_z - 1,)),
            dma((n_z - 1,)),
            dma((n_z - 1,)),
            dma,
            dma,
            dma,
            dma((2, row_blocks)),
        ],
        compiler_params=pltpu.CompilerParams(
            collective_id=bit, has_side_effects=True, vmem_limit_bytes=48 * 2**20
        ),
    )(cols_t, places, hidden, out_grad, weights, momentum)


def body(hidden, out_grad, weights, momentum, block_cols, step_number):
    level_count = lax.axis_size("replica").bit_length() - 1
    chosen_bit = step_number[0] % level_count
    branches = [
        functools.partial(fused_step, bit, lax.axis_size("tensor"))
        for bit in range(level_count)
    ]
    per_row = block_cols.shape[1]
    col_blocks = out_grad.shape[1] // weights.shape[2]
    slots = jnp.arange(per_row, dtype=jnp.int32)
    hit = block_cols.T[:, :, None] == jnp.arange(col_blocks, dtype=jnp.int32)
    places = per_row + jnp.sum(jnp.where(hit, slots[:, None, None] - per_row, 0), axis=0)
    outputs, weight_new, moment_new = lax.switch(
        chosen_bit,
        branches,
        hidden,
        out_grad,
        weights[0],
        momentum[0],
        block_cols.T,
        places.astype(jnp.int32),
    )
    return outputs, weight_new[None], moment_new[None]


def solution(mesh):
    return jax.shard_map(
        body,
        mesh=mesh,
        in_specs=(
            P("replica", "tensor"),
            P(("replica", "tensor"), None),
            P("replica", "tensor", None, None),
            P("replica", "tensor", None, None),
            P("tensor", None),
            P(),
        ),
        out_specs=(
            P(("replica", "tensor"), None),
            P("replica", "tensor", None, None),
            P("replica", "tensor", None, None),
        ),
        check_vma=False,
    )
```

```python
import functools

import jax
import jax.numpy as jnp
from jax import lax
from jax.experimental import pallas as pl
from jax.experimental.pallas import tpu as pltpu
from jax.sharding import PartitionSpec as P

LAMBDA_DC = 1.0
MOMENT_DECAY = 0.9
LEARN_RATE = 0.2
MESH = pl.DeviceIdType.MESH


def step_kernel(
    bit,
    n_z,
    scale,
    cols_ref,
    hid_hbm,
    og_hbm,
    w_hbm,
    m_hbm,
    out_v,
    nw_v,
    nm_v,
    hid_v,
    w_v,
    m_v,
    wp_v,
    mp_v,
    sec_v,
    sec_c,
    wd_v,
    part_v,
    rs_v,
    keep_v,
    ysend_v,
    yrecv_v,
    inv_ref,
    ld_sem,
    g_send,
    g_recv,
    ag_send,
    ag_recv,
    rs_send,
    rs_recv,
    y_send,
    y_recv,
):
    row_blocks, block, width = w_hbm.shape
    rows_here, model_width = og_hbm.shape
    col_blocks = model_width // block
    per_row = width // block
    replica = lax.axis_index("replica")
    tensor = lax.axis_index("tensor")
    z, y_lo = tensor // 2, tensor % 2
    low = (replica // (1 << bit)) % 2
    partner = replica + (1 - 2 * low) * (1 << bit)
    y_mate = z * 2 + (1 - y_lo)
    z_mates = [lax.rem(z + d, n_z) for d in range(1, n_z)]

    loads = [
        pltpu.make_async_copy(hid_hbm, hid_v, ld_sem.at[0]),
        pltpu.make_async_copy(
            og_hbm, sec_v.at[pl.ds(tensor * rows_here, rows_here)], ld_sem.at[1]
        ),
        pltpu.make_async_copy(m_hbm, m_v, ld_sem.at[2]),
    ]
    loads += [
        pltpu.make_async_copy(
            w_hbm.at[:, :, pl.ds(k * block, block)], w_v.at[:, k], ld_sem.at[3 + k]
        )
        for k in range(per_row)
    ]
    if bit == 0:
        for copy in loads:
            copy.start()

    barrier = pltpu.get_barrier_semaphore()
    pl.semaphore_signal(
        barrier, inc=1, device_id={"replica": partner}, device_id_type=MESH
    )
    for peer in [y_mate] + [zz * 2 + y_lo for zz in z_mates]:
        pl.semaphore_signal(
            barrier, inc=1, device_id={"tensor": peer}, device_id_type=MESH
        )
    pl.semaphore_wait(barrier, n_z + 1)

    def gather_copy(src, owner, peer, slot, recv):
        return pltpu.make_async_remote_copy(
            src_ref=src,
            dst_ref=sec_v.at[pl.ds(owner * rows_here, rows_here)],
            send_sem=ag_send.at[slot],
            recv_sem=ag_recv.at[recv],
            device_id={"tensor": peer},
            device_id_type=MESH,
        )

    first = [gather_copy(og_hbm, tensor, y_mate, 0, 0)]
    for d in range(1, n_z):
        first.append(
            gather_copy(og_hbm, tensor, z_mates[d - 1] * 2 + y_lo, d, 2 * d - 1)
        )

    def start_gather():
        for copy in first:
            copy.start()

    def gossip(r):
        pair = []
        for a, (src, dst) in enumerate(((w_hbm, wp_v), (m_hbm, mp_v))):
            pair.append(
                pltpu.make_async_remote_copy(
                    src_ref=src.at[r],
                    dst_ref=dst.at[r],
                    send_sem=g_send.at[a, r],
                    recv_sem=g_recv.at[a, r],
                    device_id={"replica": partner},
                    device_id_type=MESH,
                )
            )
        return pair

    early = row_blocks // 2

    def start_gossip(r, carry):
        for copy in gossip(r):
            copy.start()
        return carry

    if bit == 0:
        start_gather()
        lax.fori_loop(0, early, start_gossip, 0)
    else:
        lax.fori_loop(0, 1, start_gossip, 0)
        start_gather()
        lax.fori_loop(1, early, start_gossip, 0)
        for copy in loads:
            copy.start()

    for r in range(row_blocks):
        w_v[r, per_row] = jnp.zeros((block, block), w_v.dtype)

    def locate(r, carry):
        cols = [cols_ref[k, r] for k in range(per_row)]
        for c in range(col_blocks):
            at = jnp.int32(per_row)
            for k in range(per_row):
                at = jnp.where(cols[k] == c, jnp.int32(k), at)
            inv_ref[r, c] = at
        return carry

    lax.fori_loop(0, row_blocks, locate, 0)

    loads[0].wait()
    for copy in loads[3:]:
        copy.wait()
    pair_width = 2 * block

    def forward(c, carry):
        for r in range(row_blocks):
            for h in range(2):
                wd_v[pl.ds(r * block, block), pl.ds(h * block, block)] = w_v[
                    r, inv_ref[r, c * 2 + h]
                ]
        product = jnp.dot(hid_v[...], wd_v[...], preferred_element_type=jnp.float32)
        part_v[:, pl.ds(pl.multiple_of(c * pair_width, pair_width), pair_width)] = (
            product * scale
        ).astype(part_v.dtype)
        return carry

    lax.fori_loop(0, col_blocks // 2, forward, 0)

    first[0].wait_recv()
    second = []
    for d in range(1, n_z):
        second.append(
            gather_copy(
                sec_v.at[pl.ds(y_mate * rows_here, rows_here)],
                y_mate,
                z_mates[d - 1] * 2 + y_lo,
                n_z - 1 + d,
                2 * d,
            )
        )
    for copy in second:
        copy.start()

    z_rows = 2 * rows_here
    scatter = []
    for d in range(1, n_z):
        scatter.append(
            pltpu.make_async_remote_copy(
                src_ref=part_v.at[pl.ds(z_mates[d - 1] * z_rows, z_rows)],
                dst_ref=rs_v.at[d - 1],
                send_sem=rs_send.at[d - 1],
                recv_sem=rs_recv.at[d - 1],
                device_id={"tensor": z_mates[d - 1] * 2 + y_lo},
                device_id_type=MESH,
            )
        )
    for copy in scatter:
        copy.start()
    lax.fori_loop(early, row_blocks, start_gossip, 0)

    loads[1].wait()
    loads[2].wait()
    for copy in first[1:] + second:
        copy.wait_recv()
    for c in range(col_blocks):
        sec_c[c] = sec_v[:, pl.ds(c * block, block)]

    def update(r, carry):
        hid_t = hid_v[:, pl.ds(pl.multiple_of(r * block, block), block)].T
        for copy in gossip(r):
            copy.wait_recv()
        for k in range(0, per_row, 2):
            picked = [sec_c[cols_ref[k + h, r]] for h in range(2)]
            at = pl.ds(k * block, pair_width)
            grad = scale * jnp.dot(
                hid_t,
                jnp.concatenate(picked, axis=1),
                preferred_element_type=jnp.float32,
            )
            own_w = jnp.concatenate([w_v[r, k], w_v[r, k + 1]], axis=1)
            own_w = own_w.astype(jnp.float32)
            mean_w = 0.5 * (own_w + wp_v[r, :, at].astype(jnp.float32))
            mean_m = 0.5 * (
                m_v[r, :, at].astype(jnp.float32) + mp_v[r, :, at].astype(jnp.float32)
            )
            corrected = grad + LAMBDA_DC * grad * grad * (mean_w - own_w)
            moment = MOMENT_DECAY * mean_m + corrected
            nm_v[r, :, at] = moment.astype(nm_v.dtype)
            nw_v[r, :, at] = (mean_w - LEARN_RATE * moment).astype(nw_v.dtype)
        return carry

    stop_a = row_blocks // 4
    stop_b = row_blocks - 3
    lax.fori_loop(0, stop_a, update, 0)

    for copy in scatter:
        copy.wait_recv()
    other = 1 - y_lo
    for dst, row in ((ysend_v, other), (keep_v, y_lo)):
        total = part_v[pl.ds(z * z_rows + row * rows_here, rows_here), :].astype(
            jnp.float32
        )
        for d in range(1, n_z):
            total += rs_v[d - 1, pl.ds(row * rows_here, rows_here), :].astype(
                jnp.float32
            )
        dst[...] = total.astype(dst.dtype)
    to_mate = pltpu.make_async_remote_copy(
        src_ref=ysend_v,
        dst_ref=yrecv_v,
        send_sem=y_send,
        recv_sem=y_recv,
        device_id={"tensor": y_mate},
        device_id_type=MESH,
    )
    to_mate.start()

    lax.fori_loop(stop_a, stop_b, update, 0)
    to_mate.wait_recv()
    out_v[...] = (keep_v[...] + yrecv_v[...].astype(jnp.float32)).astype(out_v.dtype)
    lax.fori_loop(stop_b, row_blocks, update, 0)

    def finish(r, carry):
        for copy in gossip(r):
            copy.wait_send()
        return carry

    lax.fori_loop(0, row_blocks, finish, 0)
    for copy in first + second + scatter + [to_mate]:
        copy.wait_send()


def store_kernel(*refs):
    sems = refs[-1]
    count = len(refs) // 2
    copies = []
    for i, (src, dst) in enumerate(zip(refs[:count], refs[count : 2 * count])):
        half = src.shape[0] // 2
        for h in range(2):
            copies.append(
                pltpu.make_async_copy(
                    src.at[pl.ds(h * half, half)],
                    dst.at[pl.ds(h * half, half)],
                    sems.at[i, h],
                )
            )
    for copy in copies:
        copy.start()
    for copy in copies:
        copy.wait()


def store(*arrays):
    count = len(arrays)
    return pl.pallas_call(
        store_kernel,
        name="store_results",
        out_shape=tuple(jax.ShapeDtypeStruct(a.shape, a.dtype) for a in arrays),
        in_specs=[pl.BlockSpec(memory_space=pltpu.VMEM)] * count,
        out_specs=(pl.BlockSpec(memory_space=pl.ANY),) * count,
        scratch_shapes=[pltpu.SemaphoreType.DMA((count, 2))],
        compiler_params=pltpu.CompilerParams(vmem_limit_bytes=2**20),
    )(*arrays)


def fused_step(bit, n_tensor, hidden, out_grad, weights, momentum, cols_t):
    token_count, unit_count = hidden.shape
    rows_here, model_width = out_grad.shape
    row_blocks, block, width = weights.shape
    n_z = n_tensor // 2
    scale = (4.0 / (unit_count * n_tensor)) ** 0.5
    b16, f32 = jnp.bfloat16, jnp.float32
    dma = pltpu.SemaphoreType.DMA
    any_spec = pl.BlockSpec(memory_space=pl.ANY)
    results = pl.pallas_call(
        functools.partial(step_kernel, bit, n_z, scale),
        name=f"gossip_step_{bit}",
        out_shape=(
            pltpu.VMEM(out_grad.shape, b16),
            pltpu.VMEM(weights.shape, b16),
            pltpu.VMEM(momentum.shape, b16),
        ),
        in_specs=[pl.BlockSpec(memory_space=pltpu.SMEM)] + [any_spec] * 4,
        out_specs=(pl.BlockSpec(memory_space=pltpu.VMEM),) * 3,
        scratch_shapes=[
            pltpu.VMEM((token_count, unit_count), b16),
            pltpu.VMEM((row_blocks, width // block + 1, block, block), b16),
            pltpu.VMEM((row_blocks, block, width), b16),
            pltpu.VMEM((row_blocks, block, width), b16),
            pltpu.VMEM((row_blocks, block, width), b16),
            pltpu.VMEM((token_count, model_width), b16),
            pltpu.VMEM((model_width // block, token_count, block), b16),
            pltpu.VMEM((unit_count, 2 * block), b16),
            pltpu.VMEM((token_count, model_width), b16),
            pltpu.VMEM((n_z - 1, 2 * rows_here, model_width), b16),
            pltpu.VMEM((rows_here, model_width), f32),
            pltpu.VMEM((rows_here, model_width), b16),
            pltpu.VMEM((rows_here, model_width), b16),
            pltpu.SMEM((row_blocks, model_width // block), jnp.int32),
            dma((3 + width // block,)),
            dma((2, row_blocks)),
            dma((2, row_blocks)),
            dma((2 * n_z - 1,)),
            dma((2 * n_z - 1,)),
            dma((n_z - 1,)),
            dma((n_z - 1,)),
            dma,
            dma,
        ],
        compiler_params=pltpu.CompilerParams(
            collective_id=bit, has_side_effects=True, vmem_limit_bytes=48 * 2**20
        ),
    )(cols_t, hidden, out_grad, weights, momentum)
    return store(*results)


def body(hidden, out_grad, weights, momentum, block_cols, step_number):
    level_count = lax.axis_size("replica").bit_length() - 1
    chosen_bit = step_number[0] % level_count
    branches = [
        functools.partial(fused_step, bit, lax.axis_size("tensor"))
        for bit in range(level_count)
    ]
    outputs, weight_new, moment_new = lax.switch(
        chosen_bit,
        branches,
        hidden,
        out_grad,
        weights[0],
        momentum[0],
        block_cols.T,
    )
    return outputs, weight_new[None], moment_new[None]


def solution(mesh):
    return jax.shard_map(
        body,
        mesh=mesh,
        in_specs=(
            P("replica", "tensor"),
            P(("replica", "tensor"), None),
            P("replica", "tensor", None, None),
            P("replica", "tensor", None, None),
            P("tensor", None),
            P(),
        ),
        out_specs=(
            P(("replica", "tensor"), None),
            P("replica", "tensor", None, None),
            P("replica", "tensor", None, None),
        ),
        check_vma=False,
    )
```

```python
import functools

import jax
import jax.numpy as jnp
from jax import lax
from jax.experimental import pallas as pl
from jax.experimental.pallas import tpu as pltpu
from jax.sharding import PartitionSpec as P

LAMBDA_DC = 1.0
MOMENT_DECAY = 0.9
LEARN_RATE = 0.2
MESH = pl.DeviceIdType.MESH


def step_kernel(
    bit,
    over_y,
    n_z,
    scale,
    cols_ref,
    hid_hbm,
    og_hbm,
    w_hbm,
    m_hbm,
    out_v,
    nw_v,
    nm_v,
    hid_v,
    w_v,
    m_v,
    wp_v,
    mp_v,
    sec_v,
    sec_c,
    wd_v,
    part_v,
    rs_v,
    keep_v,
    ysend_v,
    yrecv_v,
    cross_v,
    fold_v,
    inv_ref,
    ld_sem,
    g_send,
    g_recv,
    ag_send,
    ag_recv,
    rs_send,
    rs_recv,
    y_send,
    y_recv,
    c_send,
    c_recv,
):
    row_blocks, block, width = w_hbm.shape
    rows_here, model_width = og_hbm.shape
    col_blocks = model_width // block
    per_row = width // block
    replica = lax.axis_index("replica")
    tensor = lax.axis_index("tensor")
    z, y_lo = tensor // 2, tensor % 2
    low = (replica // (1 << bit)) % 2
    partner = replica + (1 - 2 * low) * (1 << bit)
    y_mate = z * 2 + (1 - y_lo)
    z_mates = [lax.rem(z + d, n_z) for d in range(1, n_z)]

    loads = [
        pltpu.make_async_copy(hid_hbm, hid_v, ld_sem.at[0]),
        pltpu.make_async_copy(
            og_hbm, sec_v.at[pl.ds(tensor * rows_here, rows_here)], ld_sem.at[1]
        ),
        pltpu.make_async_copy(m_hbm, m_v, ld_sem.at[2]),
    ]
    loads += [
        pltpu.make_async_copy(
            w_hbm.at[:, :, pl.ds(k * block, block)], w_v.at[:, k], ld_sem.at[3 + k]
        )
        for k in range(per_row)
    ]
    if bit == 0:
        for copy in loads:
            copy.start()

    barrier = pltpu.get_barrier_semaphore()
    pl.semaphore_signal(
        barrier, inc=1, device_id={"replica": partner}, device_id_type=MESH
    )
    for peer in [y_mate] + [zz * 2 + y_lo for zz in z_mates]:
        pl.semaphore_signal(
            barrier, inc=1, device_id={"tensor": peer}, device_id_type=MESH
        )
    pl.semaphore_wait(barrier, n_z + 1)

    def gather_copy(src, owner, peer, slot, recv):
        return pltpu.make_async_remote_copy(
            src_ref=src,
            dst_ref=sec_v.at[pl.ds(owner * rows_here, rows_here)],
            send_sem=ag_send.at[slot],
            recv_sem=ag_recv.at[recv],
            device_id={"tensor": peer},
            device_id_type=MESH,
        )

    first = [gather_copy(og_hbm, tensor, y_mate, 0, 0)]
    for d in range(1, n_z):
        first.append(
            gather_copy(og_hbm, tensor, z_mates[d - 1] * 2 + y_lo, d, 2 * d - 1)
        )

    def start_gather():
        for copy in first:
            copy.start()

    def gossip(r):
        pair = []
        for a, (src, dst) in enumerate(((w_hbm, wp_v), (m_hbm, mp_v))):
            pair.append(
                pltpu.make_async_remote_copy(
                    src_ref=src.at[r],
                    dst_ref=dst.at[r],
                    send_sem=g_send.at[a, r],
                    recv_sem=g_recv.at[a, r],
                    device_id={"replica": partner},
                    device_id_type=MESH,
                )
            )
        return pair

    early = row_blocks // 2

    def start_gossip(r, carry):
        for copy in gossip(r):
            copy.start()
        return carry

    if bit == 0:
        start_gather()
        lax.fori_loop(0, early, start_gossip, 0)
    else:
        lax.fori_loop(0, 1, start_gossip, 0)
        start_gather()
        lax.fori_loop(1, early, start_gossip, 0)
        for copy in loads:
            copy.start()

    for r in range(row_blocks):
        w_v[r, per_row] = jnp.zeros((block, block), w_v.dtype)

    def locate(r, carry):
        cols = [cols_ref[k, r] for k in range(per_row)]
        for c in range(col_blocks):
            at = jnp.int32(per_row)
            for k in range(per_row):
                at = jnp.where(cols[k] == c, jnp.int32(k), at)
            inv_ref[r, c] = at
        return carry

    lax.fori_loop(0, row_blocks, locate, 0)

    loads[0].wait()
    for copy in loads[3:]:
        copy.wait()
    pair_width = 2 * block

    def forward(c, carry):
        for r in range(row_blocks):
            for h in range(2):
                wd_v[pl.ds(r * block, block), pl.ds(h * block, block)] = w_v[
                    r, inv_ref[r, c * 2 + h]
                ]
        product = jnp.dot(hid_v[...], wd_v[...], preferred_element_type=jnp.float32)
        part_v[:, pl.ds(pl.multiple_of(c * pair_width, pair_width), pair_width)] = (
            product * scale
        ).astype(part_v.dtype)
        return carry

    lax.fori_loop(0, col_blocks // 2, forward, 0)

    first[0].wait_recv()
    second = []
    half = n_z // 2
    for d in range(1, n_z):
        if over_y and d == half:
            continue
        second.append(
            gather_copy(
                sec_v.at[pl.ds(y_mate * rows_here, rows_here)],
                y_mate,
                z_mates[d - 1] * 2 + y_lo,
                n_z - 1 + d,
                2 * d,
            )
        )
    for copy in second:
        copy.start()

    z_rows = 2 * rows_here
    far = z_mates[half - 1]

    def part_rows(zz, row, count):
        return part_v.at[pl.ds(zz * z_rows + row * rows_here, count)]

    def scatter_copy(d):
        whole = not (over_y and d == half)
        return pltpu.make_async_remote_copy(
            src_ref=part_rows(z_mates[d - 1], 0, z_rows) if whole else fold_v,
            dst_ref=rs_v.at[d - 1] if whole else rs_v.at[d - 1, pl.ds(0, rows_here)],
            send_sem=rs_send.at[d - 1],
            recv_sem=rs_recv.at[d - 1],
            device_id={"tensor": z_mates[d - 1] * 2 + y_lo},
            device_id_type=MESH,
        )

    scatter = [scatter_copy(d) for d in range(1, n_z)]
    other = 1 - y_lo
    cross = []
    if over_y:
        cross.append(
            pltpu.make_async_remote_copy(
                src_ref=part_rows(far, other, rows_here),
                dst_ref=cross_v,
                send_sem=c_send,
                recv_sem=c_recv,
                device_id={"tensor": y_mate},
                device_id_type=MESH,
            )
        )
        cross[0].start()
    for d in range(1, n_z):
        if not (over_y and d == half):
            scatter[d - 1].start()
    lax.fori_loop(early, row_blocks, start_gossip, 0)

    loads[1].wait()
    loads[2].wait()
    third = []
    if over_y:
        cross[0].wait_recv()
        fold_v[...] = (
            part_rows(far, y_lo, rows_here)[...].astype(jnp.float32)
            + cross_v[...].astype(jnp.float32)
        ).astype(fold_v.dtype)
        first[half].wait_recv()
        third.append(
            gather_copy(
                sec_v.at[pl.ds((far * 2 + y_lo) * rows_here, rows_here)],
                far * 2 + y_lo,
                y_mate,
                n_z - 1 + half,
                2 * half,
            )
        )
        third[0].start()
        scatter[half - 1].start()
    for d in range(1, n_z):
        if not (over_y and d == half):
            first[d].wait_recv()
    for copy in second + third:
        copy.wait_recv()
    for c in range(col_blocks):
        sec_c[c] = sec_v[:, pl.ds(c * block, block)]

    def update(r, carry):
        hid_t = hid_v[:, pl.ds(pl.multiple_of(r * block, block), block)].T
        for copy in gossip(r):
            copy.wait_recv()
        for k in range(0, per_row, 2):
            picked = [sec_c[cols_ref[k + h, r]] for h in range(2)]
            at = pl.ds(k * block, pair_width)
            grad = scale * jnp.dot(
                hid_t,
                jnp.concatenate(picked, axis=1),
                preferred_element_type=jnp.float32,
            )
            own_w = jnp.concatenate([w_v[r, k], w_v[r, k + 1]], axis=1)
            own_w = own_w.astype(jnp.float32)
            mean_w = 0.5 * (own_w + wp_v[r, :, at].astype(jnp.float32))
            mean_m = 0.5 * (
                m_v[r, :, at].astype(jnp.float32) + mp_v[r, :, at].astype(jnp.float32)
            )
            corrected = grad + LAMBDA_DC * grad * grad * (mean_w - own_w)
            moment = MOMENT_DECAY * mean_m + corrected
            nm_v[r, :, at] = moment.astype(nm_v.dtype)
            nw_v[r, :, at] = (mean_w - LEARN_RATE * moment).astype(nw_v.dtype)
        return carry

    stop_a = row_blocks // (2 if bit == 0 else 4)
    stop_b = row_blocks - 3
    lax.fori_loop(0, stop_a, update, 0)

    for copy in scatter:
        copy.wait_recv()
    for dst, row in ((ysend_v, other), (keep_v, y_lo)):
        total = part_rows(z, row, rows_here)[...].astype(jnp.float32)
        for d in range(1, n_z):
            at = row * rows_here
            if over_y and d == half:
                if dst is ysend_v:
                    continue
                at = 0
            total += rs_v[d - 1, pl.ds(at, rows_here), :].astype(jnp.float32)
        dst[...] = total.astype(dst.dtype)
    to_mate = pltpu.make_async_remote_copy(
        src_ref=ysend_v,
        dst_ref=yrecv_v,
        send_sem=y_send,
        recv_sem=y_recv,
        device_id={"tensor": y_mate},
        device_id_type=MESH,
    )
    to_mate.start()

    lax.fori_loop(stop_a, stop_b, update, 0)
    to_mate.wait_recv()
    out_v[...] = (keep_v[...] + yrecv_v[...].astype(jnp.float32)).astype(out_v.dtype)
    lax.fori_loop(stop_b, row_blocks, update, 0)

    def finish(r, carry):
        for copy in gossip(r):
            copy.wait_send()
        return carry

    lax.fori_loop(0, row_blocks, finish, 0)
    for copy in first + second + third + cross + scatter + [to_mate]:
        copy.wait_send()


def store_kernel(*refs):
    sems = refs[-1]
    count = len(refs) // 2
    copies = []
    for i, (src, dst) in enumerate(zip(refs[:count], refs[count : 2 * count])):
        half = src.shape[0] // 2
        for h in range(2):
            copies.append(
                pltpu.make_async_copy(
                    src.at[pl.ds(h * half, half)],
                    dst.at[pl.ds(h * half, half)],
                    sems.at[i, h],
                )
            )
    for copy in copies:
        copy.start()
    for copy in copies:
        copy.wait()


def store(*arrays):
    count = len(arrays)
    return pl.pallas_call(
        store_kernel,
        name="store_results",
        out_shape=tuple(jax.ShapeDtypeStruct(a.shape, a.dtype) for a in arrays),
        in_specs=[pl.BlockSpec(memory_space=pltpu.VMEM)] * count,
        out_specs=(pl.BlockSpec(memory_space=pl.ANY),) * count,
        scratch_shapes=[pltpu.SemaphoreType.DMA((count, 2))],
        compiler_params=pltpu.CompilerParams(vmem_limit_bytes=2**20),
    )(*arrays)


def fused_step(bit, over_y, n_tensor, hidden, out_grad, weights, momentum, cols_t):
    token_count, unit_count = hidden.shape
    rows_here, model_width = out_grad.shape
    row_blocks, block, width = weights.shape
    n_z = n_tensor // 2
    scale = (4.0 / (unit_count * n_tensor)) ** 0.5
    b16, f32 = jnp.bfloat16, jnp.float32
    dma = pltpu.SemaphoreType.DMA
    any_spec = pl.BlockSpec(memory_space=pl.ANY)
    results = pl.pallas_call(
        functools.partial(step_kernel, bit, over_y, n_z, scale),
        name=f"gossip_step_{bit}",
        out_shape=(
            pltpu.VMEM(out_grad.shape, b16),
            pltpu.VMEM(weights.shape, b16),
            pltpu.VMEM(momentum.shape, b16),
        ),
        in_specs=[pl.BlockSpec(memory_space=pltpu.SMEM)] + [any_spec] * 4,
        out_specs=(pl.BlockSpec(memory_space=pltpu.VMEM),) * 3,
        scratch_shapes=[
            pltpu.VMEM((token_count, unit_count), b16),
            pltpu.VMEM((row_blocks, width // block + 1, block, block), b16),
            pltpu.VMEM((row_blocks, block, width), b16),
            pltpu.VMEM((row_blocks, block, width), b16),
            pltpu.VMEM((row_blocks, block, width), b16),
            pltpu.VMEM((token_count, model_width), b16),
            pltpu.VMEM((model_width // block, token_count, block), b16),
            pltpu.VMEM((unit_count, 2 * block), b16),
            pltpu.VMEM((token_count, model_width), b16),
            pltpu.VMEM((n_z - 1, 2 * rows_here, model_width), b16),
            pltpu.VMEM((rows_here, model_width), f32),
            pltpu.VMEM((rows_here, model_width), b16),
            pltpu.VMEM((rows_here, model_width), b16),
            pltpu.VMEM((rows_here, model_width), b16),
            pltpu.VMEM((rows_here, model_width), b16),
            pltpu.SMEM((row_blocks, model_width // block), jnp.int32),
            dma((3 + width // block,)),
            dma((2, row_blocks)),
            dma((2, row_blocks)),
            dma((2 * n_z - 1,)),
            dma((2 * n_z - 1,)),
            dma((n_z - 1,)),
            dma((n_z - 1,)),
            dma,
            dma,
            dma,
            dma,
        ],
        compiler_params=pltpu.CompilerParams(
            collective_id=bit, has_side_effects=True, vmem_limit_bytes=48 * 2**20
        ),
    )(cols_t, hidden, out_grad, weights, momentum)
    return store(*results)


def body(hidden, out_grad, weights, momentum, block_cols, step_number):
    level_count = lax.axis_size("replica").bit_length() - 1
    chosen_bit = step_number[0] % level_count
    branches = [
        functools.partial(fused_step, bit, bit < level_count - 1, lax.axis_size("tensor"))
        for bit in range(level_count)
    ]
    outputs, weight_new, moment_new = lax.switch(
        chosen_bit,
        branches,
        hidden,
        out_grad,
        weights[0],
        momentum[0],
        block_cols.T,
    )
    return outputs, weight_new[None], moment_new[None]


def solution(mesh):
    return jax.shard_map(
        body,
        mesh=mesh,
        in_specs=(
            P("replica", "tensor"),
            P(("replica", "tensor"), None),
            P("replica", "tensor", None, None),
            P("replica", "tensor", None, None),
            P("tensor", None),
            P(),
        ),
        out_specs=(
            P(("replica", "tensor"), None),
            P("replica", "tensor", None, None),
            P("replica", "tensor", None, None),
        ),
        check_vma=False,
    )
```

```python
import functools

import jax
import jax.numpy as jnp
from jax import lax
from jax.experimental import pallas as pl
from jax.experimental.pallas import tpu as pltpu
from jax.sharding import PartitionSpec as P

LAMBDA_DC = 1.0
MOMENT_DECAY = 0.9
LEARN_RATE = 0.2
MESH = pl.DeviceIdType.MESH


def step_kernel(
    bit,
    over_y,
    n_z,
    scale,
    cols_ref,
    hid_hbm,
    og_hbm,
    w_hbm,
    m_hbm,
    out_v,
    nw_v,
    nm_v,
    hid_v,
    w_v,
    m_v,
    wp_v,
    mp_v,
    sec_v,
    sec_c,
    wd_v,
    part_v,
    rs_v,
    keep_v,
    ysend_v,
    yrecv_v,
    cross_v,
    fold_v,
    hop_v,
    inv_ref,
    ld_sem,
    g_send,
    g_recv,
    ag_send,
    ag_recv,
    rs_send,
    rs_recv,
    y_send,
    y_recv,
    c_send,
    c_recv,
    h_send,
    h_recv,
):
    row_blocks, block, width = w_hbm.shape
    rows_here, model_width = og_hbm.shape
    col_blocks = model_width // block
    per_row = width // block
    replica = lax.axis_index("replica")
    tensor = lax.axis_index("tensor")
    z, y_lo = tensor // 2, tensor % 2
    low = (replica // (1 << bit)) % 2
    partner = replica + (1 - 2 * low) * (1 << bit)
    y_mate = z * 2 + (1 - y_lo)
    z_mates = [lax.rem(z + d, n_z) for d in range(1, n_z)]

    loads = [
        pltpu.make_async_copy(hid_hbm, hid_v, ld_sem.at[0]),
        pltpu.make_async_copy(
            og_hbm, sec_v.at[pl.ds(tensor * rows_here, rows_here)], ld_sem.at[1]
        ),
        pltpu.make_async_copy(m_hbm, m_v, ld_sem.at[2]),
    ]
    loads += [
        pltpu.make_async_copy(
            w_hbm.at[:, :, pl.ds(k * block, block)], w_v.at[:, k], ld_sem.at[3 + k]
        )
        for k in range(per_row)
    ]
    if bit == 0:
        for copy in loads:
            copy.start()

    barrier = pltpu.get_barrier_semaphore()
    pl.semaphore_signal(
        barrier, inc=1, device_id={"replica": partner}, device_id_type=MESH
    )
    half = n_z // 2
    met = [zz for d, zz in enumerate(z_mates, 1) if d != half or not over_y]
    for peer in [y_mate] + [zz * 2 + y_lo for zz in met]:
        pl.semaphore_signal(
            barrier, inc=1, device_id={"tensor": peer}, device_id_type=MESH
        )
    pl.semaphore_wait(barrier, 2 + len(met))

    def gather_copy(src, owner, peer, slot, recv):
        return pltpu.make_async_remote_copy(
            src_ref=src,
            dst_ref=sec_v.at[pl.ds(owner * rows_here, rows_here)],
            send_sem=ag_send.at[slot],
            recv_sem=ag_recv.at[recv],
            device_id={"tensor": peer},
            device_id_type=MESH,
        )

    far = z_mates[half - 1]
    near = [d for d in range(1, n_z) if d != half]
    first = [gather_copy(og_hbm, tensor, y_mate, 0, 0)]
    for d in near:
        first.append(
            gather_copy(og_hbm, tensor, z_mates[d - 1] * 2 + y_lo, d, 2 * d - 1)
        )
    half_rows = rows_here // 2
    relays = []
    for i, d in enumerate(near):
        owner = z_mates[n_z - d - 1] * 2 + y_lo
        rows = sec_v.at[pl.ds(owner * rows_here + i * half_rows, half_rows)]
        slot = (half, 2 * n_z - 1)[i]
        relays.append(
            pltpu.make_async_remote_copy(
                src_ref=rows,
                dst_ref=rows,
                send_sem=ag_send.at[slot],
                recv_sem=ag_recv.at[(2 * half - 1, 2 * n_z - 1)[i]],
                device_id={"tensor": z_mates[d - 1] * 2 + y_lo},
                device_id_type=MESH,
            )
        )

    def start_gather():
        for copy in first:
            copy.start()

    def gossip(r):
        pair = []
        for a, (src, dst) in enumerate(((w_hbm, wp_v), (m_hbm, mp_v))):
            pair.append(
                pltpu.make_async_remote_copy(
                    src_ref=src.at[r],
                    dst_ref=dst.at[r],
                    send_sem=g_send.at[a, r],
                    recv_sem=g_recv.at[a, r],
                    device_id={"replica": partner},
                    device_id_type=MESH,
                )
            )
        return pair

    early = row_blocks // 2

    def start_gossip(r, carry):
        for copy in gossip(r):
            copy.start()
        return carry

    if bit == 0:
        start_gather()
        lax.fori_loop(0, early, start_gossip, 0)
    else:
        lax.fori_loop(0, 1, start_gossip, 0)
        start_gather()
        lax.fori_loop(1, early, start_gossip, 0)
        for copy in loads:
            copy.start()

    for r in range(row_blocks):
        w_v[r, per_row] = jnp.zeros((block, block), w_v.dtype)

    def locate(r, carry):
        cols = [cols_ref[k, r] for k in range(per_row)]
        for c in range(col_blocks):
            at = jnp.int32(per_row)
            for k in range(per_row):
                at = jnp.where(cols[k] == c, jnp.int32(k), at)
            inv_ref[r, c] = at
        return carry

    lax.fori_loop(0, row_blocks, locate, 0)

    loads[0].wait()
    for copy in loads[3:]:
        copy.wait()
    pair_width = 2 * block

    def forward(c, carry):
        for r in range(row_blocks):
            for h in range(2):
                wd_v[pl.ds(r * block, block), pl.ds(h * block, block)] = w_v[
                    r, inv_ref[r, c * 2 + h]
                ]
        product = jnp.dot(hid_v[...], wd_v[...], preferred_element_type=jnp.float32)
        part_v[:, pl.ds(pl.multiple_of(c * pair_width, pair_width), pair_width)] = (
            product * scale
        ).astype(part_v.dtype)
        return carry

    lax.fori_loop(0, col_blocks // 4, forward, 0)

    second = []
    for d in range(1, n_z):
        if over_y and d == half:
            continue
        second.append(
            gather_copy(
                sec_v.at[pl.ds(y_mate * rows_here, rows_here)],
                y_mate,
                z_mates[d - 1] * 2 + y_lo,
                n_z - 1 + d,
                2 * d,
            )
        )
    for copy in first:
        copy.wait_recv()
    for copy in relays + second:
        copy.start()
    lax.fori_loop(col_blocks // 4, col_blocks // 2, forward, 0)
    lax.fori_loop(early, row_blocks, start_gossip, 0)

    z_rows = 2 * rows_here

    def part_rows(zz, row, count):
        return part_v.at[pl.ds(zz * z_rows + row * rows_here, count)]

    def scatter_copy(d):
        return pltpu.make_async_remote_copy(
            src_ref=part_rows(z_mates[d - 1], 0, z_rows),
            dst_ref=rs_v.at[d - 1],
            send_sem=rs_send.at[d - 1],
            recv_sem=rs_recv.at[d - 1],
            device_id={"tensor": z_mates[d - 1] * 2 + y_lo},
            device_id_type=MESH,
        )

    def hop_copy(i, src, dst, sem):
        return pltpu.make_async_remote_copy(
            src_ref=src,
            dst_ref=dst,
            send_sem=h_send.at[sem],
            recv_sem=h_recv.at[sem],
            device_id={"tensor": z_mates[near[i] - 1] * 2 + y_lo},
            device_id_type=MESH,
        )

    scatter = [scatter_copy(d) for d in (near if over_y else range(1, n_z))]
    hops = []
    for i in range(2 if over_y else 0):
        rows = pl.ds(i * half_rows, half_rows)
        hops.append(hop_copy(i, fold_v.at[rows], hop_v.at[i], i))
    for i in range(2 if over_y else 0):
        rows = pl.ds(i * half_rows, half_rows)
        hops.append(hop_copy(i, hop_v.at[i], rs_v.at[half - 1, rows], 2 + i))
    other = 1 - y_lo
    cross = []
    if over_y:
        cross.append(
            pltpu.make_async_remote_copy(
                src_ref=part_rows(far, other, rows_here),
                dst_ref=cross_v,
                send_sem=c_send,
                recv_sem=c_recv,
                device_id={"tensor": y_mate},
                device_id_type=MESH,
            )
        )
        cross[0].start()
    for copy in scatter:
        copy.start()

    loads[1].wait()
    loads[2].wait()
    third = []
    if over_y:
        cross[0].wait_recv()
        fold_v[...] = (
            part_rows(far, y_lo, rows_here)[...].astype(jnp.float32)
            + cross_v[...].astype(jnp.float32)
        ).astype(fold_v.dtype)
        for copy in relays:
            copy.wait_recv()
        third.append(
            gather_copy(
                sec_v.at[pl.ds((far * 2 + y_lo) * rows_here, rows_here)],
                far * 2 + y_lo,
                y_mate,
                n_z - 1 + half,
                2 * half,
            )
        )
        third[0].start()
        for copy in hops[:2]:
            copy.start()
    else:
        for copy in relays:
            copy.wait_recv()
    for copy in second + third:
        copy.wait_recv()
    for c in range(col_blocks):
        sec_c[c] = sec_v[:, pl.ds(c * block, block)]

    def update(r, carry):
        hid_t = hid_v[:, pl.ds(pl.multiple_of(r * block, block), block)].T
        for copy in gossip(r):
            copy.wait_recv()
        for k in range(0, per_row, 2):
            picked = [sec_c[cols_ref[k + h, r]] for h in range(2)]
            at = pl.ds(k * block, pair_width)
            grad = scale * jnp.dot(
                hid_t,
                jnp.concatenate(picked, axis=1),
                preferred_element_type=jnp.float32,
            )
            own_w = jnp.concatenate([w_v[r, k], w_v[r, k + 1]], axis=1)
            own_w = own_w.astype(jnp.float32)
            mean_w = 0.5 * (own_w + wp_v[r, :, at].astype(jnp.float32))
            mean_m = 0.5 * (
                m_v[r, :, at].astype(jnp.float32) + mp_v[r, :, at].astype(jnp.float32)
            )
            corrected = grad + LAMBDA_DC * grad * grad * (mean_w - own_w)
            moment = MOMENT_DECAY * mean_m + corrected
            nm_v[r, :, at] = moment.astype(nm_v.dtype)
            nw_v[r, :, at] = (mean_w - LEARN_RATE * moment).astype(nw_v.dtype)
        return carry

    stop_a = row_blocks // (2 if bit == 0 else 4)
    stop_b = row_blocks - (0 if bit == 0 else 3)
    lax.fori_loop(0, stop_a, update, 0)

    def reduce(dst, row, steps):
        total = part_rows(z, row, rows_here)[...].astype(jnp.float32)
        for d in steps:
            at = 0 if over_y and d == half else row * rows_here
            total += rs_v[d - 1, pl.ds(at, rows_here), :].astype(jnp.float32)
        dst[...] = total.astype(dst.dtype)

    for copy in scatter:
        copy.wait_recv()
    reduce(ysend_v, other, near if over_y else range(1, n_z))
    if not over_y:
        reduce(keep_v, y_lo, range(1, n_z))
    else:
        reduce(keep_v, y_lo, near)
    to_mate = pltpu.make_async_remote_copy(
        src_ref=ysend_v,
        dst_ref=yrecv_v,
        send_sem=y_send,
        recv_sem=y_recv,
        device_id={"tensor": y_mate},
        device_id_type=MESH,
    )
    to_mate.start()
    for i in range(len(hops) // 2):
        hops[i].wait_recv()
        hops[2 + i].start()

    lax.fori_loop(stop_a, stop_b, update, 0)
    total = keep_v[...]
    if over_y:
        for copy in hops[2:]:
            copy.wait_recv()
        total += rs_v[half - 1, pl.ds(0, rows_here), :].astype(jnp.float32)
    to_mate.wait_recv()
    out_v[...] = (total + yrecv_v[...].astype(jnp.float32)).astype(out_v.dtype)
    lax.fori_loop(stop_b, row_blocks, update, 0)

    def finish(r, carry):
        for copy in gossip(r):
            copy.wait_send()
        return carry

    lax.fori_loop(0, row_blocks, finish, 0)
    for copy in first + relays + second + third + cross + scatter + hops + [to_mate]:
        copy.wait_send()


def store_kernel(*refs):
    sems = refs[-1]
    count = len(refs) // 2
    copies = []
    for i, (src, dst) in enumerate(zip(refs[:count], refs[count : 2 * count])):
        half = src.shape[0] // 2
        for h in range(2):
            copies.append(
                pltpu.make_async_copy(
                    src.at[pl.ds(h * half, half)],
                    dst.at[pl.ds(h * half, half)],
                    sems.at[i, h],
                )
            )
    for copy in copies:
        copy.start()
    for copy in copies:
        copy.wait()


def store(*arrays):
    count = len(arrays)
    return pl.pallas_call(
        store_kernel,
        name="store_results",
        out_shape=tuple(jax.ShapeDtypeStruct(a.shape, a.dtype) for a in arrays),
        in_specs=[pl.BlockSpec(memory_space=pltpu.VMEM)] * count,
        out_specs=(pl.BlockSpec(memory_space=pl.ANY),) * count,
        scratch_shapes=[pltpu.SemaphoreType.DMA((count, 2))],
        compiler_params=pltpu.CompilerParams(vmem_limit_bytes=2**20),
    )(*arrays)


def fused_step(bit, over_y, n_tensor, hidden, out_grad, weights, momentum, cols_t):
    token_count, unit_count = hidden.shape
    rows_here, model_width = out_grad.shape
    row_blocks, block, width = weights.shape
    n_z = n_tensor // 2
    scale = (4.0 / (unit_count * n_tensor)) ** 0.5
    b16, f32 = jnp.bfloat16, jnp.float32
    dma = pltpu.SemaphoreType.DMA
    any_spec = pl.BlockSpec(memory_space=pl.ANY)
    results = pl.pallas_call(
        functools.partial(step_kernel, bit, over_y, n_z, scale),
        name=f"gossip_step_{bit}",
        out_shape=(
            pltpu.VMEM(out_grad.shape, b16),
            pltpu.VMEM(weights.shape, b16),
            pltpu.VMEM(momentum.shape, b16),
        ),
        in_specs=[pl.BlockSpec(memory_space=pltpu.SMEM)] + [any_spec] * 4,
        out_specs=(pl.BlockSpec(memory_space=pltpu.VMEM),) * 3,
        scratch_shapes=[
            pltpu.VMEM((token_count, unit_count), b16),
            pltpu.VMEM((row_blocks, width // block + 1, block, block), b16),
            pltpu.VMEM((row_blocks, block, width), b16),
            pltpu.VMEM((row_blocks, block, width), b16),
            pltpu.VMEM((row_blocks, block, width), b16),
            pltpu.VMEM((token_count, model_width), b16),
            pltpu.VMEM((model_width // block, token_count, block), b16),
            pltpu.VMEM((unit_count, 2 * block), b16),
            pltpu.VMEM((token_count, model_width), b16),
            pltpu.VMEM((n_z - 1, 2 * rows_here, model_width), b16),
            pltpu.VMEM((rows_here, model_width), f32),
            pltpu.VMEM((rows_here, model_width), b16),
            pltpu.VMEM((rows_here, model_width), b16),
            pltpu.VMEM((rows_here, model_width), b16),
            pltpu.VMEM((rows_here, model_width), b16),
            pltpu.VMEM((2, rows_here // 2, model_width), b16),
            pltpu.SMEM((row_blocks, model_width // block), jnp.int32),
            dma((3 + width // block,)),
            dma((2, row_blocks)),
            dma((2, row_blocks)),
            dma((2 * n_z,)),
            dma((2 * n_z,)),
            dma((n_z - 1,)),
            dma((n_z - 1,)),
            dma,
            dma,
            dma,
            dma,
            dma((4,)),
            dma((4,)),
        ],
        compiler_params=pltpu.CompilerParams(
            collective_id=bit, has_side_effects=True, vmem_limit_bytes=48 * 2**20
        ),
    )(cols_t, hidden, out_grad, weights, momentum)
    return store(*results)


def body(hidden, out_grad, weights, momentum, block_cols, step_number):
    level_count = lax.axis_size("replica").bit_length() - 1
    chosen_bit = step_number[0] % level_count
    branches = [
        functools.partial(fused_step, bit, bit < level_count - 1, lax.axis_size("tensor"))
        for bit in range(level_count)
    ]
    outputs, weight_new, moment_new = lax.switch(
        chosen_bit,
        branches,
        hidden,
        out_grad,
        weights[0],
        momentum[0],
        block_cols.T,
    )
    return outputs, weight_new[None], moment_new[None]


def solution(mesh):
    return jax.shard_map(
        body,
        mesh=mesh,
        in_specs=(
            P("replica", "tensor"),
            P(("replica", "tensor"), None),
            P("replica", "tensor", None, None),
            P("replica", "tensor", None, None),
            P("tensor", None),
            P(),
        ),
        out_specs=(
            P(("replica", "tensor"), None),
            P("replica", "tensor", None, None),
            P("replica", "tensor", None, None),
        ),
        check_vma=False,
    )
```

```python
import functools

import jax
import jax.numpy as jnp
from jax import lax
from jax.experimental import pallas as pl
from jax.experimental.pallas import tpu as pltpu
from jax.sharding import PartitionSpec as P

LAMBDA_DC = 1.0
MOMENT_DECAY = 0.9
LEARN_RATE = 0.2
MESH = pl.DeviceIdType.MESH


def step_kernel(
    bit,
    over_y,
    n_z,
    scale,
    cols_hbm,
    hid_hbm,
    og_hbm,
    w_hbm,
    m_hbm,
    out_v,
    nw_v,
    nm_v,
    hid_v,
    w_v,
    m_v,
    wp_v,
    mp_v,
    sec_v,
    sec_c,
    wd_v,
    part_v,
    rs_v,
    keep_v,
    ysend_v,
    yrecv_v,
    cross_v,
    fold_v,
    hop_v,
    grad_v,
    cols_ref,
    inv_ref,
    ld_sem,
    g_send,
    g_recv,
    ag_send,
    ag_recv,
    rs_send,
    rs_recv,
    y_send,
    y_recv,
    c_send,
    c_recv,
    h_send,
    h_recv,
):
    row_blocks, block, width = w_hbm.shape
    rows_here, model_width = og_hbm.shape
    col_blocks = model_width // block
    per_row = width // block
    replica = lax.axis_index("replica")
    tensor = lax.axis_index("tensor")
    z, y_lo = tensor // 2, tensor % 2
    low = (replica // (1 << bit)) % 2
    partner = replica + (1 - 2 * low) * (1 << bit)
    y_mate = z * 2 + (1 - y_lo)
    z_mates = [lax.rem(z + d, n_z) for d in range(1, n_z)]

    loads = [
        pltpu.make_async_copy(hid_hbm, hid_v, ld_sem.at[0]),
        pltpu.make_async_copy(
            og_hbm, sec_v.at[pl.ds(tensor * rows_here, rows_here)], ld_sem.at[1]
        ),
        pltpu.make_async_copy(m_hbm, m_v, ld_sem.at[2]),
    ]
    loads += [
        pltpu.make_async_copy(
            w_hbm.at[:, :, pl.ds(k * block, block)], w_v.at[:, k], ld_sem.at[3 + k]
        )
        for k in range(per_row)
    ]
    table = pltpu.make_async_copy(cols_hbm, cols_ref, ld_sem.at[3 + per_row])
    if bit == 0:
        for copy in [table] + loads:
            copy.start()

    barrier = pltpu.get_barrier_semaphore()
    pl.semaphore_signal(
        barrier, inc=1, device_id={"replica": partner}, device_id_type=MESH
    )
    half = n_z // 2
    met = [zz for d, zz in enumerate(z_mates, 1) if d != half or not over_y]
    for peer in [y_mate] + [zz * 2 + y_lo for zz in met]:
        pl.semaphore_signal(
            barrier, inc=1, device_id={"tensor": peer}, device_id_type=MESH
        )
    pl.semaphore_wait(barrier, 2 + len(met))

    def gather_copy(src, owner, peer, slot, recv):
        return pltpu.make_async_remote_copy(
            src_ref=src,
            dst_ref=sec_v.at[pl.ds(owner * rows_here, rows_here)],
            send_sem=ag_send.at[slot],
            recv_sem=ag_recv.at[recv],
            device_id={"tensor": peer},
            device_id_type=MESH,
        )

    far = z_mates[half - 1]
    near = [d for d in range(1, n_z) if d != half]
    first = [gather_copy(og_hbm, tensor, y_mate, 0, 0)]
    for d in near:
        first.append(
            gather_copy(og_hbm, tensor, z_mates[d - 1] * 2 + y_lo, d, 2 * d - 1)
        )
    half_rows = rows_here // 2
    relays = []
    for i, d in enumerate(near):
        owner = z_mates[n_z - d - 1] * 2 + y_lo
        rows = sec_v.at[pl.ds(owner * rows_here + i * half_rows, half_rows)]
        slot = (half, 2 * n_z - 1)[i]
        relays.append(
            pltpu.make_async_remote_copy(
                src_ref=rows,
                dst_ref=rows,
                send_sem=ag_send.at[slot],
                recv_sem=ag_recv.at[(2 * half - 1, 2 * n_z - 1)[i]],
                device_id={"tensor": z_mates[d - 1] * 2 + y_lo},
                device_id_type=MESH,
            )
        )

    def start_gather():
        for copy in first:
            copy.start()

    def gossip(r):
        pair = []
        for a, (src, dst) in enumerate(((w_hbm, wp_v), (m_hbm, mp_v))):
            pair.append(
                pltpu.make_async_remote_copy(
                    src_ref=src.at[r],
                    dst_ref=dst.at[r],
                    send_sem=g_send.at[a, r],
                    recv_sem=g_recv.at[a, r],
                    device_id={"replica": partner},
                    device_id_type=MESH,
                )
            )
        return pair

    early = row_blocks // 2

    def start_gossip(r, carry):
        for copy in gossip(r):
            copy.start()
        return carry

    if bit == 0:
        start_gather()
        lax.fori_loop(0, early, start_gossip, 0)
    else:
        lax.fori_loop(0, 1, start_gossip, 0)
        start_gather()
        lax.fori_loop(1, early, start_gossip, 0)
        for copy in [table] + loads:
            copy.start()

    for r in range(row_blocks):
        w_v[r, per_row] = jnp.zeros((block, block), w_v.dtype)

    def locate(r, carry):
        cols = [cols_ref[k, r] for k in range(per_row)]
        for c in range(col_blocks):
            at = jnp.int32(per_row)
            for k in range(per_row):
                at = jnp.where(cols[k] == c, jnp.int32(k), at)
            inv_ref[r, c] = at
        return carry

    table.wait()
    lax.fori_loop(0, row_blocks, locate, 0)

    loads[0].wait()
    for copy in loads[3:]:
        copy.wait()
    pair_width = 2 * block

    def forward(c, carry):
        for r in range(row_blocks):
            for h in range(2):
                wd_v[pl.ds(r * block, block), pl.ds(h * block, block)] = w_v[
                    r, inv_ref[r, c * 2 + h]
                ]
        product = jnp.dot(hid_v[...], wd_v[...], preferred_element_type=jnp.float32)
        part_v[:, pl.ds(pl.multiple_of(c * pair_width, pair_width), pair_width)] = (
            product * scale
        ).astype(part_v.dtype)
        return carry

    lax.fori_loop(0, col_blocks // 4, forward, 0)

    second = []
    for d in range(1, n_z):
        if over_y and d == half:
            continue
        second.append(
            gather_copy(
                sec_v.at[pl.ds(y_mate * rows_here, rows_here)],
                y_mate,
                z_mates[d - 1] * 2 + y_lo,
                n_z - 1 + d,
                2 * d,
            )
        )
    for copy in first:
        copy.wait_recv()
    for copy in relays + second:
        copy.start()
    lax.fori_loop(col_blocks // 4, col_blocks // 2, forward, 0)
    lax.fori_loop(early, row_blocks, start_gossip, 0)

    z_rows = 2 * rows_here

    def part_rows(zz, row, count):
        return part_v.at[pl.ds(zz * z_rows + row * rows_here, count)]

    def scatter_copy(d):
        return pltpu.make_async_remote_copy(
            src_ref=part_rows(z_mates[d - 1], 0, z_rows),
            dst_ref=rs_v.at[d - 1],
            send_sem=rs_send.at[d - 1],
            recv_sem=rs_recv.at[d - 1],
            device_id={"tensor": z_mates[d - 1] * 2 + y_lo},
            device_id_type=MESH,
        )

    def hop_copy(i, src, dst, sem):
        return pltpu.make_async_remote_copy(
            src_ref=src,
            dst_ref=dst,
            send_sem=h_send.at[sem],
            recv_sem=h_recv.at[sem],
            device_id={"tensor": z_mates[near[i] - 1] * 2 + y_lo},
            device_id_type=MESH,
        )

    scatter = [scatter_copy(d) for d in (near if over_y else range(1, n_z))]
    hops = []
    for i in range(2 if over_y else 0):
        rows = pl.ds(i * half_rows, half_rows)
        hops.append(hop_copy(i, fold_v.at[rows], hop_v.at[i], i))
    for i in range(2 if over_y else 0):
        rows = pl.ds(i * half_rows, half_rows)
        hops.append(hop_copy(i, hop_v.at[i], rs_v.at[half - 1, rows], 2 + i))
    other = 1 - y_lo
    cross = []
    if over_y:
        cross.append(
            pltpu.make_async_remote_copy(
                src_ref=part_rows(far, other, rows_here),
                dst_ref=cross_v,
                send_sem=c_send,
                recv_sem=c_recv,
                device_id={"tensor": y_mate},
                device_id_type=MESH,
            )
        )
        cross[0].start()
    for copy in scatter:
        copy.start()

    loads[1].wait()
    loads[2].wait()
    third = []
    if over_y:
        cross[0].wait_recv()
        fold_v[...] = (
            part_rows(far, y_lo, rows_here)[...].astype(jnp.float32)
            + cross_v[...].astype(jnp.float32)
        ).astype(fold_v.dtype)
        for copy in relays:
            copy.wait_recv()
        third.append(
            gather_copy(
                sec_v.at[pl.ds((far * 2 + y_lo) * rows_here, rows_here)],
                far * 2 + y_lo,
                y_mate,
                n_z - 1 + half,
                2 * half,
            )
        )
        third[0].start()
        for copy in hops[:2]:
            copy.start()
    else:
        for copy in relays:
            copy.wait_recv()
    for copy in second + third:
        copy.wait_recv()
    for c in range(col_blocks):
        sec_c[c] = sec_v[:, pl.ds(c * block, block)]

    def update(r, carry):
        hid_t = hid_v[:, pl.ds(pl.multiple_of(r * block, block), block)].T
        for k in range(0, per_row, 2):
            picked = [sec_c[cols_ref[k + h, r]] for h in range(2)]
            grad_v[:, pl.ds(k * block, pair_width)] = scale * jnp.dot(
                hid_t,
                jnp.concatenate(picked, axis=1),
                preferred_element_type=jnp.float32,
            )
        for copy in gossip(r):
            copy.wait_recv()
        for k in range(0, per_row, 2):
            at = pl.ds(k * block, pair_width)
            grad = grad_v[:, at]
            own_w = jnp.concatenate([w_v[r, k], w_v[r, k + 1]], axis=1)
            own_w = own_w.astype(jnp.float32)
            mean_w = 0.5 * (own_w + wp_v[r, :, at].astype(jnp.float32))
            mean_m = 0.5 * (
                m_v[r, :, at].astype(jnp.float32) + mp_v[r, :, at].astype(jnp.float32)
            )
            corrected = grad + LAMBDA_DC * grad * grad * (mean_w - own_w)
            moment = MOMENT_DECAY * mean_m + corrected
            nm_v[r, :, at] = moment.astype(nm_v.dtype)
            nw_v[r, :, at] = (mean_w - LEARN_RATE * moment).astype(nw_v.dtype)
        return carry

    stop_a = row_blocks // (2 if bit == 0 else 4)
    stop_b = row_blocks - (0 if bit == 0 else 3)
    lax.fori_loop(0, stop_a, update, 0)

    def reduce(dst, row, steps):
        total = part_rows(z, row, rows_here)[...].astype(jnp.float32)
        for d in steps:
            at = 0 if over_y and d == half else row * rows_here
            total += rs_v[d - 1, pl.ds(at, rows_here), :].astype(jnp.float32)
        dst[...] = total.astype(dst.dtype)

    for copy in scatter:
        copy.wait_recv()
    reduce(ysend_v, other, near if over_y else range(1, n_z))
    if not over_y:
        reduce(keep_v, y_lo, range(1, n_z))
    else:
        reduce(keep_v, y_lo, near)
    to_mate = pltpu.make_async_remote_copy(
        src_ref=ysend_v,
        dst_ref=yrecv_v,
        send_sem=y_send,
        recv_sem=y_recv,
        device_id={"tensor": y_mate},
        device_id_type=MESH,
    )
    to_mate.start()
    for i in range(len(hops) // 2):
        hops[i].wait_recv()
        hops[2 + i].start()

    lax.fori_loop(stop_a, stop_b, update, 0)
    total = keep_v[...]
    if over_y:
        for copy in hops[2:]:
            copy.wait_recv()
        total += rs_v[half - 1, pl.ds(0, rows_here), :].astype(jnp.float32)
    to_mate.wait_recv()
    out_v[...] = (total + yrecv_v[...].astype(jnp.float32)).astype(out_v.dtype)
    lax.fori_loop(stop_b, row_blocks, update, 0)

    def finish(r, carry):
        for copy in gossip(r):
            copy.wait_send()
        return carry

    lax.fori_loop(0, row_blocks, finish, 0)
    for copy in first + relays + second + third + cross + scatter + hops + [to_mate]:
        copy.wait_send()


def store_kernel(*refs):
    sems = refs[-1]
    count = len(refs) // 2
    copies = []
    for i, (src, dst) in enumerate(zip(refs[:count], refs[count : 2 * count])):
        size = src.shape[0] // 2
        for h in range(2):
            at = pl.ds(h * size, size)
            copies.append(
                pltpu.make_async_copy(src.at[at], dst.at[at], sems.at[i, h])
            )
    for copy in copies:
        copy.start()
    for copy in copies:
        copy.wait()


def store(*arrays):
    count = len(arrays)
    return pl.pallas_call(
        store_kernel,
        name="store_results",
        out_shape=tuple(jax.ShapeDtypeStruct(a.shape, a.dtype) for a in arrays),
        in_specs=[pl.BlockSpec(memory_space=pltpu.VMEM)] * count,
        out_specs=(pl.BlockSpec(memory_space=pl.ANY),) * count,
        scratch_shapes=[pltpu.SemaphoreType.DMA((count, 2))],
        compiler_params=pltpu.CompilerParams(vmem_limit_bytes=2**20),
    )(*arrays)


def fused_step(bit, over_y, n_tensor, hidden, out_grad, weights, momentum, cols_t):
    token_count, unit_count = hidden.shape
    rows_here, model_width = out_grad.shape
    row_blocks, block, width = weights.shape
    n_z = n_tensor // 2
    scale = (4.0 / (unit_count * n_tensor)) ** 0.5
    b16, f32 = jnp.bfloat16, jnp.float32
    dma = pltpu.SemaphoreType.DMA
    any_spec = pl.BlockSpec(memory_space=pl.ANY)
    results = pl.pallas_call(
        functools.partial(step_kernel, bit, over_y, n_z, scale),
        name=f"gossip_step_{bit}",
        out_shape=(
            pltpu.VMEM(out_grad.shape, b16),
            pltpu.VMEM(weights.shape, b16),
            pltpu.VMEM(momentum.shape, b16),
        ),
        in_specs=[any_spec] * 5,
        out_specs=(pl.BlockSpec(memory_space=pltpu.VMEM),) * 3,
        scratch_shapes=[
            pltpu.VMEM((token_count, unit_count), b16),
            pltpu.VMEM((row_blocks, width // block + 1, block, block), b16),
            pltpu.VMEM((row_blocks, block, width), b16),
            pltpu.VMEM((row_blocks, block, width), b16),
            pltpu.VMEM((row_blocks, block, width), b16),
            pltpu.VMEM((token_count, model_width), b16),
            pltpu.VMEM((model_width // block, token_count, block), b16),
            pltpu.VMEM((unit_count, 2 * block), b16),
            pltpu.VMEM((token_count, model_width), b16),
            pltpu.VMEM((n_z - 1, 2 * rows_here, model_width), b16),
            pltpu.VMEM((rows_here, model_width), f32),
            pltpu.VMEM((rows_here, model_width), b16),
            pltpu.VMEM((rows_here, model_width), b16),
            pltpu.VMEM((rows_here, model_width), b16),
            pltpu.VMEM((rows_here, model_width), b16),
            pltpu.VMEM((2, rows_here // 2, model_width), b16),
            pltpu.VMEM((block, width), f32),
            pltpu.SMEM(cols_t.shape, jnp.int32),
            pltpu.SMEM((row_blocks, model_width // block), jnp.int32),
            dma((4 + width // block,)),
            dma((2, row_blocks)),
            dma((2, row_blocks)),
            dma((2 * n_z,)),
            dma((2 * n_z,)),
            dma((n_z - 1,)),
            dma((n_z - 1,)),
            dma,
            dma,
            dma,
            dma,
            dma((4,)),
            dma((4,)),
        ],
        compiler_params=pltpu.CompilerParams(
            collective_id=bit, has_side_effects=True, vmem_limit_bytes=48 * 2**20
        ),
    )(cols_t, hidden, out_grad, weights, momentum)
    return store(*results)


def body(hidden, out_grad, weights, momentum, block_cols, step_number):
    level_count = lax.axis_size("replica").bit_length() - 1
    chosen_bit = step_number[0] % level_count
    branches = [
        functools.partial(fused_step, bit, bit < level_count - 1, lax.axis_size("tensor"))
        for bit in range(level_count)
    ]
    outputs, weight_new, moment_new = lax.switch(
        chosen_bit,
        branches,
        hidden,
        out_grad,
        weights[0],
        momentum[0],
        block_cols.T,
    )
    return outputs, weight_new[None], moment_new[None]


def solution(mesh):
    return jax.shard_map(
        body,
        mesh=mesh,
        in_specs=(
            P("replica", "tensor"),
            P(("replica", "tensor"), None),
            P("replica", "tensor", None, None),
            P("replica", "tensor", None, None),
            P("tensor", None),
            P(),
        ),
        out_specs=(
            P(("replica", "tensor"), None),
            P("replica", "tensor", None, None),
            P("replica", "tensor", None, None),
        ),
        check_vma=False,
    )
```

```python
import functools

import jax
import jax.numpy as jnp
from jax import lax
from jax.experimental import pallas as pl
from jax.experimental.pallas import tpu as pltpu
from jax.sharding import PartitionSpec as P

LAMBDA_DC = 1.0
MOMENT_DECAY = 0.9
LEARN_RATE = 0.2
MESH = pl.DeviceIdType.MESH


def step_kernel(
    bit,
    over_y,
    n_z,
    scale,
    cols_hbm,
    hid_hbm,
    og_hbm,
    w_hbm,
    m_hbm,
    out_v,
    nw_v,
    nm_v,
    hid_v,
    w_v,
    m_v,
    wp_v,
    mp_v,
    sec_v,
    sec_c,
    wd_v,
    part_v,
    rs_v,
    keep_v,
    ysend_v,
    yrecv_v,
    cross_v,
    fold_v,
    hop_v,
    grad_v,
    cols_ref,
    inv_ref,
    ld_sem,
    g_send,
    g_recv,
    ag_send,
    ag_recv,
    rs_send,
    rs_recv,
    y_send,
    y_recv,
    c_send,
    c_recv,
    h_send,
    h_recv,
):
    row_blocks, block, width = w_hbm.shape
    rows_here, model_width = og_hbm.shape
    col_blocks = model_width // block
    per_row = width // block
    replica = lax.axis_index("replica")
    tensor = lax.axis_index("tensor")
    z, y_lo = tensor // 2, tensor % 2
    low = (replica // (1 << bit)) % 2
    partner = replica + (1 - 2 * low) * (1 << bit)
    y_mate = z * 2 + (1 - y_lo)
    z_mates = [lax.rem(z + d, n_z) for d in range(1, n_z)]

    loads = [
        pltpu.make_async_copy(hid_hbm, hid_v, ld_sem.at[0]),
        pltpu.make_async_copy(
            og_hbm, sec_v.at[pl.ds(tensor * rows_here, rows_here)], ld_sem.at[1]
        ),
        pltpu.make_async_copy(m_hbm, m_v, ld_sem.at[2]),
    ]
    loads += [
        pltpu.make_async_copy(
            w_hbm.at[:, :, pl.ds(k * block, block)], w_v.at[:, k], ld_sem.at[3 + k]
        )
        for k in range(per_row)
    ]
    table = pltpu.make_async_copy(cols_hbm, cols_ref, ld_sem.at[3 + per_row])
    if bit == 0:
        for copy in [table] + loads:
            copy.start()

    barrier = pltpu.get_barrier_semaphore()
    pl.semaphore_signal(
        barrier, inc=1, device_id={"replica": partner}, device_id_type=MESH
    )
    half = n_z // 2
    met = [zz for d, zz in enumerate(z_mates, 1) if d != half or not over_y]
    for peer in [y_mate] + [zz * 2 + y_lo for zz in met]:
        pl.semaphore_signal(
            barrier, inc=1, device_id={"tensor": peer}, device_id_type=MESH
        )
    pl.semaphore_wait(barrier, 2 + len(met))

    def gather_copy(src, owner, peer, slot, recv):
        return pltpu.make_async_remote_copy(
            src_ref=src,
            dst_ref=sec_v.at[pl.ds(owner * rows_here, rows_here)],
            send_sem=ag_send.at[slot],
            recv_sem=ag_recv.at[recv],
            device_id={"tensor": peer},
            device_id_type=MESH,
        )

    far = z_mates[half - 1]
    near = [d for d in range(1, n_z) if d != half]
    first = [gather_copy(og_hbm, tensor, y_mate, 0, 0)]
    for d in near:
        first.append(
            gather_copy(og_hbm, tensor, z_mates[d - 1] * 2 + y_lo, d, 2 * d - 1)
        )
    half_rows = rows_here // 2
    relays = []
    for i, d in enumerate(near):
        owner = z_mates[n_z - d - 1] * 2 + y_lo
        rows = sec_v.at[pl.ds(owner * rows_here + i * half_rows, half_rows)]
        slot = (half, 2 * n_z - 1)[i]
        relays.append(
            pltpu.make_async_remote_copy(
                src_ref=rows,
                dst_ref=rows,
                send_sem=ag_send.at[slot],
                recv_sem=ag_recv.at[(2 * half - 1, 2 * n_z - 1)[i]],
                device_id={"tensor": z_mates[d - 1] * 2 + y_lo},
                device_id_type=MESH,
            )
        )

    def start_gather():
        for copy in first:
            copy.start()

    def gossip(r):
        pair = []
        for a, (src, dst) in enumerate(((w_hbm, wp_v), (m_hbm, mp_v))):
            pair.append(
                pltpu.make_async_remote_copy(
                    src_ref=src.at[r],
                    dst_ref=dst.at[r],
                    send_sem=g_send.at[a, r],
                    recv_sem=g_recv.at[a, r],
                    device_id={"replica": partner},
                    device_id_type=MESH,
                )
            )
        return pair

    early = row_blocks // 2

    def start_gossip(r, carry):
        for copy in gossip(r):
            copy.start()
        return carry

    if bit == 0:
        start_gather()
        lax.fori_loop(0, early, start_gossip, 0)
    else:
        lax.fori_loop(0, 1, start_gossip, 0)
        start_gather()
        lax.fori_loop(1, early, start_gossip, 0)
        for copy in [table] + loads:
            copy.start()

    for r in range(row_blocks):
        w_v[r, per_row] = jnp.zeros((block, block), w_v.dtype)

    def locate(r, carry):
        cols = [cols_ref[k, r] for k in range(per_row)]
        for c in range(col_blocks):
            at = jnp.int32(per_row)
            for k in range(per_row):
                at = jnp.where(cols[k] == c, jnp.int32(k), at)
            inv_ref[r, c] = at
        return carry

    table.wait()
    lax.fori_loop(0, row_blocks, locate, 0)

    loads[0].wait()
    for copy in loads[3:]:
        copy.wait()
    pair_width = 2 * block

    def forward(c, carry):
        for r in range(row_blocks):
            for h in range(2):
                wd_v[pl.ds(r * block, block), pl.ds(h * block, block)] = w_v[
                    r, inv_ref[r, c * 2 + h]
                ]
        product = jnp.dot(hid_v[...], wd_v[...], preferred_element_type=jnp.float32)
        part_v[:, pl.ds(pl.multiple_of(c * pair_width, pair_width), pair_width)] = (
            product * scale
        ).astype(part_v.dtype)
        return carry

    lax.fori_loop(0, col_blocks // 4, forward, 0)

    second = []
    for d in range(1, n_z):
        if over_y and d == half:
            continue
        second.append(
            gather_copy(
                sec_v.at[pl.ds(y_mate * rows_here, rows_here)],
                y_mate,
                z_mates[d - 1] * 2 + y_lo,
                n_z - 1 + d,
                2 * d,
            )
        )
    for copy in first:
        copy.wait_recv()
    for copy in relays + second:
        copy.start()
    lax.fori_loop(col_blocks // 4, col_blocks // 2, forward, 0)
    lax.fori_loop(early, row_blocks, start_gossip, 0)

    z_rows = 2 * rows_here

    def part_rows(zz, row, count):
        return part_v.at[pl.ds(zz * z_rows + row * rows_here, count)]

    def scatter_copy(d):
        return pltpu.make_async_remote_copy(
            src_ref=part_rows(z_mates[d - 1], 0, z_rows),
            dst_ref=rs_v.at[d - 1],
            send_sem=rs_send.at[d - 1],
            recv_sem=rs_recv.at[d - 1],
            device_id={"tensor": z_mates[d - 1] * 2 + y_lo},
            device_id_type=MESH,
        )

    def hop_copy(i, src, dst, sem):
        return pltpu.make_async_remote_copy(
            src_ref=src,
            dst_ref=dst,
            send_sem=h_send.at[sem],
            recv_sem=h_recv.at[sem],
            device_id={"tensor": z_mates[near[i] - 1] * 2 + y_lo},
            device_id_type=MESH,
        )

    scatter = [scatter_copy(d) for d in (near if over_y else range(1, n_z))]
    hops = []
    for i in range(2 if over_y else 0):
        rows = pl.ds(i * half_rows, half_rows)
        hops.append(hop_copy(i, fold_v.at[rows], hop_v.at[i], i))
    for i in range(2 if over_y else 0):
        rows = pl.ds(i * half_rows, half_rows)
        hops.append(hop_copy(i, hop_v.at[i], rs_v.at[half - 1, rows], 2 + i))
    other = 1 - y_lo
    cross = []
    if over_y:
        cross.append(
            pltpu.make_async_remote_copy(
                src_ref=part_rows(far, other, rows_here),
                dst_ref=cross_v,
                send_sem=c_send,
                recv_sem=c_recv,
                device_id={"tensor": y_mate},
                device_id_type=MESH,
            )
        )
        cross[0].start()
    for copy in scatter:
        copy.start()

    loads[1].wait()
    loads[2].wait()
    third = []
    if over_y:
        cross[0].wait_recv()
        fold_v[...] = (
            part_rows(far, y_lo, rows_here)[...].astype(jnp.float32)
            + cross_v[...].astype(jnp.float32)
        ).astype(fold_v.dtype)
        for copy in relays:
            copy.wait_recv()
        third.append(
            gather_copy(
                sec_v.at[pl.ds((far * 2 + y_lo) * rows_here, rows_here)],
                far * 2 + y_lo,
                y_mate,
                n_z - 1 + half,
                2 * half,
            )
        )
        third[0].start()
        for copy in hops[:2]:
            copy.start()
    else:
        for copy in relays:
            copy.wait_recv()
    for copy in second + third:
        copy.wait_recv()
    for c in range(col_blocks):
        sec_c[c] = sec_v[:, pl.ds(c * block, block)]

    def update(r, carry):
        hid_t = hid_v[:, pl.ds(pl.multiple_of(r * block, block), block)].T
        for k in range(0, per_row, 2):
            picked = [sec_c[cols_ref[k + h, r]] for h in range(2)]
            grad_v[:, pl.ds(k * block, pair_width)] = scale * jnp.dot(
                hid_t,
                jnp.concatenate(picked, axis=1),
                preferred_element_type=jnp.float32,
            )
        for copy in gossip(r):
            copy.wait()
        for k in range(0, per_row, 2):
            at = pl.ds(k * block, pair_width)
            grad = grad_v[:, at]
            own_w = jnp.concatenate([w_v[r, k], w_v[r, k + 1]], axis=1)
            own_w = own_w.astype(jnp.float32)
            mean_w = 0.5 * (own_w + wp_v[r, :, at].astype(jnp.float32))
            mean_m = 0.5 * (
                m_v[r, :, at].astype(jnp.float32) + mp_v[r, :, at].astype(jnp.float32)
            )
            corrected = grad + LAMBDA_DC * grad * grad * (mean_w - own_w)
            moment = MOMENT_DECAY * mean_m + corrected
            nm_v[r, :, at] = moment.astype(nm_v.dtype)
            nw_v[r, :, at] = (mean_w - LEARN_RATE * moment).astype(nw_v.dtype)
        return carry

    stop_a = row_blocks // (2 if bit == 0 else 4)
    stop_b = row_blocks - (0 if bit == 0 else 3)
    lax.fori_loop(0, stop_a, update, 0)

    def reduce(dst, row, steps):
        total = part_rows(z, row, rows_here)[...].astype(jnp.float32)
        for d in steps:
            at = 0 if over_y and d == half else row * rows_here
            total += rs_v[d - 1, pl.ds(at, rows_here), :].astype(jnp.float32)
        dst[...] = total.astype(dst.dtype)

    for copy in scatter:
        copy.wait_recv()
    reduce(ysend_v, other, near if over_y else range(1, n_z))
    if not over_y:
        reduce(keep_v, y_lo, range(1, n_z))
    else:
        reduce(keep_v, y_lo, near)
    to_mate = pltpu.make_async_remote_copy(
        src_ref=ysend_v,
        dst_ref=yrecv_v,
        send_sem=y_send,
        recv_sem=y_recv,
        device_id={"tensor": y_mate},
        device_id_type=MESH,
    )
    to_mate.start()
    for i in range(len(hops) // 2):
        hops[i].wait_recv()
        hops[2 + i].start()

    lax.fori_loop(stop_a, stop_b, update, 0)
    total = keep_v[...]
    if over_y:
        for copy in hops[2:]:
            copy.wait_recv()
        total += rs_v[half - 1, pl.ds(0, rows_here), :].astype(jnp.float32)
    to_mate.wait_recv()
    out_v[...] = (total + yrecv_v[...].astype(jnp.float32)).astype(out_v.dtype)
    for copy in first + relays + second + third + cross + scatter + hops + [to_mate]:
        copy.wait_send()
    lax.fori_loop(stop_b, row_blocks, update, 0)


def store_kernel(*refs):
    sems = refs[-1]
    count = len(refs) // 2
    copies = []
    for i, (src, dst) in enumerate(zip(refs[:count], refs[count : 2 * count])):
        size = src.shape[0] // 2
        for h in range(2):
            at = pl.ds(h * size, size)
            copies.append(
                pltpu.make_async_copy(src.at[at], dst.at[at], sems.at[i, h])
            )
    for copy in copies:
        copy.start()
    for copy in copies:
        copy.wait()


def store(*arrays):
    count = len(arrays)
    return pl.pallas_call(
        store_kernel,
        name="store_results",
        out_shape=tuple(jax.ShapeDtypeStruct(a.shape, a.dtype) for a in arrays),
        in_specs=[pl.BlockSpec(memory_space=pltpu.VMEM)] * count,
        out_specs=(pl.BlockSpec(memory_space=pl.ANY),) * count,
        scratch_shapes=[pltpu.SemaphoreType.DMA((count, 2))],
        compiler_params=pltpu.CompilerParams(vmem_limit_bytes=2**20),
    )(*arrays)


def fused_step(bit, over_y, n_tensor, hidden, out_grad, weights, momentum, cols_t):
    token_count, unit_count = hidden.shape
    rows_here, model_width = out_grad.shape
    row_blocks, block, width = weights.shape
    n_z = n_tensor // 2
    scale = (4.0 / (unit_count * n_tensor)) ** 0.5
    b16, f32 = jnp.bfloat16, jnp.float32
    dma = pltpu.SemaphoreType.DMA
    any_spec = pl.BlockSpec(memory_space=pl.ANY)
    results = pl.pallas_call(
        functools.partial(step_kernel, bit, over_y, n_z, scale),
        name=f"gossip_step_{bit}",
        out_shape=(
            pltpu.VMEM(out_grad.shape, b16),
            pltpu.VMEM(weights.shape, b16),
            pltpu.VMEM(momentum.shape, b16),
        ),
        in_specs=[any_spec] * 5,
        out_specs=(pl.BlockSpec(memory_space=pltpu.VMEM),) * 3,
        scratch_shapes=[
            pltpu.VMEM((token_count, unit_count), b16),
            pltpu.VMEM((row_blocks, width // block + 1, block, block), b16),
            pltpu.VMEM((row_blocks, block, width), b16),
            pltpu.VMEM((row_blocks, block, width), b16),
            pltpu.VMEM((row_blocks, block, width), b16),
            pltpu.VMEM((token_count, model_width), b16),
            pltpu.VMEM((model_width // block, token_count, block), b16),
            pltpu.VMEM((unit_count, 2 * block), b16),
            pltpu.VMEM((token_count, model_width), b16),
            pltpu.VMEM((n_z - 1, 2 * rows_here, model_width), b16),
            pltpu.VMEM((rows_here, model_width), f32),
            pltpu.VMEM((rows_here, model_width), b16),
            pltpu.VMEM((rows_here, model_width), b16),
            pltpu.VMEM((rows_here, model_width), b16),
            pltpu.VMEM((rows_here, model_width), b16),
            pltpu.VMEM((2, rows_here // 2, model_width), b16),
            pltpu.VMEM((block, width), f32),
            pltpu.SMEM(cols_t.shape, jnp.int32),
            pltpu.SMEM((row_blocks, model_width // block), jnp.int32),
            dma((4 + width // block,)),
            dma((2, row_blocks)),
            dma((2, row_blocks)),
            dma((2 * n_z,)),
            dma((2 * n_z,)),
            dma((n_z - 1,)),
            dma((n_z - 1,)),
            dma,
            dma,
            dma,
            dma,
            dma((4,)),
            dma((4,)),
        ],
        compiler_params=pltpu.CompilerParams(
            collective_id=bit, has_side_effects=True, vmem_limit_bytes=48 * 2**20
        ),
    )(cols_t, hidden, out_grad, weights, momentum)
    return store(*results)


def body(hidden, out_grad, weights, momentum, block_cols, step_number):
    level_count = lax.axis_size("replica").bit_length() - 1
    chosen_bit = step_number[0] % level_count
    branches = [
        functools.partial(fused_step, bit, bit < level_count - 1, lax.axis_size("tensor"))
        for bit in range(level_count)
    ]
    outputs, weight_new, moment_new = lax.switch(
        chosen_bit,
        branches,
        hidden,
        out_grad,
        weights[0],
        momentum[0],
        block_cols.T,
    )
    return outputs, weight_new[None], moment_new[None]


def solution(mesh):
    return jax.shard_map(
        body,
        mesh=mesh,
        in_specs=(
            P("replica", "tensor"),
            P(("replica", "tensor"), None),
            P("replica", "tensor", None, None),
            P("replica", "tensor", None, None),
            P("tensor", None),
            P(),
        ),
        out_specs=(
            P(("replica", "tensor"), None),
            P("replica", "tensor", None, None),
            P("replica", "tensor", None, None),
        ),
        check_vma=False,
    )
```
